32 devices in a mesh: groups: 2 (over y), patch: 4 (over z), head: 4 (over x, core).
Axes of the slice: x: 2, y: 2, z: 4, core: 2. Of those that a mesh axis runs over, the one named last changes fastest.
Arguments:
- queries: bfloat16 [1536, 1536], P(('groups', 'patch'), 'head'), parts along dimension 0, may hold values from -12.5 to 12.5
- fresh_keys: bfloat16 [1536, 1536], P(('groups', 'patch'), 'head'), parts along dimension 0, may hold values from -5 to 5
- fresh_values: bfloat16 [1536, 1536], P(('groups', 'patch'), 'head'), parts along dimension 0, may hold values from -6 to 6
- stale_keys: bfloat16 [1536, 1536], P(('groups', 'patch'), 'head'), parts along dimension 0, may hold values from -5 to 5
- stale_values: bfloat16 [1536, 1536], P(('groups', 'patch'), 'head'), parts along dimension 0, may hold values from -6 to 6
- out_weight: bfloat16 [1536, 5120], P('head', 'patch'), may hold values from -0.21875 to 0.21875
- gate_scale: float32 [10240], P(('groups', 'head')), parts along dimension 0, may hold values from 1 to 4
Outputs:
- branch_out: float32 [1536, 5120], P(('groups', 'patch'), 'head'), parts along dimension 0
The draws below stay inside these ranges and needn't reach their ends.
There are 2 independent parts, one for each index of `groups`. The reference program is written for one: setup_inputs(seed, part) draws one part's arguments, and reference() takes and returns one part's arrays. A program takes and returns all parts, laid end to end along the dimension named above; an argument that names none is the same for every part. Nothing has to cross between parts.
All inputs are finite; a program needn't handle non-finite values.
Results may differ from the reference program's by a relative error of at most 0.006.
Values may be sent and summed in bfloat16 or wider, within the bound.
No kernel may reach another device: no remote copies, remote signals or barrier semaphores. Data moves between devices by JAX's collectives and lax.ppermute only.
A program may use at most 64 MiB of HBM per device.

```python
import math
import jax
import jax.numpy as jnp
from jax import lax

D = 5120
HEAD_DIM = 128
HEAD_DEV = 3
TOK_DEV = 192
HEADS = 12
TOKENS = 768
N_PATCH = 4
N_HEAD = 4


def attention_inputs(key):
    feature_width = HEADS * HEAD_DIM
    key_query, key_stale, key_fresh = jax.random.split(jax.random.fold_in(key, 7), 3)
    shape = (TOKENS, feature_width)
    query_rows = 2.5 * jax.random.truncated_normal(key_query, -5.0, 5.0, shape, jnp.float32)
    stale_rows = jax.random.truncated_normal(key_stale, -5.0, 5.0, shape, jnp.float32)
    fresh_rows = jnp.clip(0.8 * stale_rows + 0.6 * jax.random.normal(key_fresh, shape, jnp.float32), -5.0, 5.0)
    return (query_rows, stale_rows, fresh_rows)


def draw_queries(key, part):
    return attention_inputs(key)[0].astype(jnp.bfloat16)


def draw_stale_keys(key, part):
    return attention_inputs(key)[1].astype(jnp.bfloat16)


def draw_fresh_keys(key, part):
    return attention_inputs(key)[2].astype(jnp.bfloat16)


def spiked(values, rng, source, target, blocks, factor):
    owner, partner = [(jnp.arange(values.shape[dim]) // (values.shape[dim] // blocks)).reshape([-1 if axis == dim else 1 for axis in range(values.ndim)]) for dim in (source, target)]
    chosen = jax.random.permutation(rng, blocks)[partner]
    strong = (owner == chosen) | (owner == (partner + blocks // 2) % blocks)
    return jnp.where(strong, factor * values, values)


def steps_of(key, shape, cuts, low, top_value):
    factor_of = 1.0
    for position, shards_of in cuts:
        steps = jax.random.uniform(jax.random.fold_in(jax.random.fold_in(key, 6), position), (shards_of,), jnp.float32, low / len(cuts), top_value / len(cuts))
        factor_of = factor_of * jnp.repeat(jnp.exp(steps), shape[position] // shards_of).reshape((-1,) + (1,) * (len(shape) - 1 - position))
    return factor_of


def normal_values(rng, dims, deviation, limit, shards=(), held_as=jnp.bfloat16):
    drawn = deviation * jax.random.normal(rng, dims, jnp.float32)
    if shards:
        drawn = drawn * steps_of(rng, dims, shards, -0.22, 0.18)
    return jnp.clip(drawn, -limit, limit).astype(held_as)


def heavy_noise(stream_key, extent, deviation, reach, pieces, heavy, held_as=jnp.bfloat16):
    entries = deviation * jax.random.normal(stream_key, extent, jnp.float32)
    if pieces:
        entries = entries * steps_of(stream_key, extent, pieces, -0.22, 0.18)
    return jnp.clip(spiked(entries, jax.random.fold_in(stream_key, 3), *heavy), -reach, reach).astype(held_as)


def setup_inputs(seed: int = 0, part: int = 0) -> dict:
    arg_keys = jax.random.split(jax.random.key(seed), 8)
    own_keys = jax.random.split(jax.random.fold_in(arg_keys[7], part), 8)
    queries = draw_queries(jax.random.fold_in(jax.random.fold_in(arg_keys[7], part), 71), part)
    fresh_keys = draw_fresh_keys(jax.random.fold_in(jax.random.fold_in(arg_keys[7], part), 71), part)
    fresh_values = normal_values(own_keys[2], (TOKENS, HEADS * HEAD_DIM), 1.0, 6.0, ((0, 4), (1, 4)))
    stale_keys = draw_stale_keys(jax.random.fold_in(jax.random.fold_in(arg_keys[7], part), 71), part)
    stale_values = normal_values(own_keys[4], (TOKENS, HEADS * HEAD_DIM), 1.0, 6.0, ((0, 4), (1, 4)))
    out_weight = heavy_noise(arg_keys[5], (HEADS * HEAD_DIM, D), (HEADS * HEAD_DIM) ** -0.5, 0.21875, ((0, 4), (1, 4)), (0, 1, 4, 2.0))
    gate_scale = jnp.clip(jnp.exp(math.log(4.0) - 1.3862944 * jax.random.uniform(own_keys[6], (D,), jnp.float32) ** steps_of(own_keys[6], (D,), ((0, 4),), -0.2, 0.2)), 1.0, 4.0)
    return dict(queries=queries, fresh_keys=fresh_keys, fresh_values=fresh_values, stale_keys=stale_keys, stale_values=stale_values, out_weight=out_weight, gate_scale=gate_scale)


def reference(queries, fresh_keys, fresh_values, stale_keys, stale_values, out_weight, gate_scale):
    query_heads = queries.astype(jnp.float32).reshape(TOKENS, HEADS, HEAD_DIM)

    def one_slab(slab):
        anchor = (slab * TOK_DEV).astype(jnp.int32)
        query_rows = lax.dynamic_slice_in_dim(query_heads, anchor, TOK_DEV, 0)
        key_rows = lax.dynamic_slice_in_dim(fresh_keys, anchor, TOK_DEV, 0)
        value_rows = lax.dynamic_slice_in_dim(fresh_values, anchor, TOK_DEV, 0)
        keys_used = lax.dynamic_update_slice_in_dim(stale_keys, key_rows, anchor, 0)
        values_used = lax.dynamic_update_slice_in_dim(stale_values, value_rows, anchor, 0)
        key_heads = keys_used.astype(jnp.float32).reshape(TOKENS, HEADS, HEAD_DIM)
        value_heads = values_used.astype(jnp.float32).reshape(TOKENS, HEADS, HEAD_DIM)
        scores = jnp.einsum("qhd,khd->hqk", query_rows, key_heads) * (HEAD_DIM ** -0.5)
        top = jnp.max(scores, axis=2)
        weights = jnp.exp(scores - top[:, :, None])
        total = jnp.sum(weights, axis=2)
        rounded = lax.optimization_barrier(weights.astype(jnp.bfloat16)).astype(jnp.float32)
        mixture = jnp.einsum("hqk,khd->qhd", rounded, value_heads)
        return (mixture / jnp.transpose(total)[:, :, None]).astype(jnp.bfloat16)

    attended = lax.map(one_slab, jnp.arange(N_PATCH, dtype=jnp.int32))
    attended = attended.reshape(TOKENS, HEADS * HEAD_DIM)
    group_width = HEAD_DEV * HEAD_DIM

    def add_group(running, group):
        anchor = (group * group_width).astype(jnp.int32)
        column_block = lax.dynamic_slice_in_dim(attended, anchor, group_width, 1)
        weight_block = lax.dynamic_slice_in_dim(out_weight, anchor, group_width, 0)
        term = jnp.dot(column_block, weight_block, preferred_element_type=jnp.float32)
        return running + term, None

    summed, unused = lax.scan(add_group, jnp.zeros((TOKENS, D), jnp.float32), jnp.arange(N_HEAD, dtype=jnp.int32))
    return gate_scale[None, :] * summed
```

```python
import functools

import jax
import jax.numpy as jnp
from jax import lax
from jax.experimental import pallas as pl
from jax.experimental.pallas import tpu as pltpu
from jax.sharding import PartitionSpec as P

HEAD_DIM = 128
MASKED = -1e30


def absorb(query, state, key, value, bias):
    scores = lax.dot_general(
        query, key, (((1,), (1,)), ((), ())), preferred_element_type=jnp.float32
    ) * HEAD_DIM ** (-0.5)
    if bias is not None:
        scores = scores + bias
    block_top = jnp.max(scores, axis=1, keepdims=True)
    top = block_top if state is None else jnp.maximum(state[0], block_top)
    weights = jnp.exp(scores - top)
    total = jnp.sum(weights, axis=1, keepdims=True)
    mixture = jnp.dot(
        weights.astype(jnp.bfloat16), value, preferred_element_type=jnp.float32
    )
    if state is not None:
        factor = jnp.exp(state[0] - top)
        total = total + state[1] * factor
        mixture = mixture + state[2] * factor
    return top, total, mixture


def head_columns(head):
    return slice(head * HEAD_DIM, (head + 1) * HEAD_DIM)


def first_kernel(count, bias_ref, q_ref, key_ref, value_ref, *refs):
    blocks, (top_ref, total_ref, mix_ref) = refs[:count], refs[count:]
    width = q_ref.shape[1]
    for head in range(width // HEAD_DIM):
        cols = head_columns(head)
        query = q_ref[:, cols]
        state = absorb(query, None, key_ref[:, cols], value_ref[:, cols], None)
        for index, block in enumerate(blocks):
            high = slice(width + head * HEAD_DIM, width + (head + 1) * HEAD_DIM)
            state = absorb(query, state, block[:, cols], block[:, high], bias_ref[index])
        top_ref[head], total_ref[head], mix_ref[:, cols] = state


def last_kernel(count, bias_ref, q_ref, top_ref, total_ref, mix_ref, *refs):
    blocks, (out_ref,) = refs[:count], refs[count:]
    width = q_ref.shape[1]
    for head in range(width // HEAD_DIM):
        cols = head_columns(head)
        query = q_ref[:, cols]
        state = (top_ref[head], total_ref[head], mix_ref[:, cols])
        for index, block in enumerate(blocks):
            high = slice(width + head * HEAD_DIM, width + (head + 1) * HEAD_DIM)
            state = absorb(query, state, block[:, cols], block[:, high], bias_ref[index])
        out_ref[:, cols] = (state[2] / state[1]).astype(out_ref.dtype)


def attention_cost(rows, width, keys):
    return pl.CostEstimate(
        flops=4 * rows * width * keys,
        transcendentals=rows * keys * (width // HEAD_DIM),
        bytes_accessed=4 * keys * width,
    )


SMEM = pl.BlockSpec(memory_space=pltpu.SMEM)
VMEM = pl.BlockSpec(memory_space=pltpu.VMEM)
PARAMS = pltpu.CompilerParams(vmem_limit_bytes=20 * 2**20)


def attend_first(queries, keys, values, blocks, bias):
    rows, width = queries.shape
    heads = width // HEAD_DIM
    count = len(blocks)
    narrow = jax.ShapeDtypeStruct((heads, rows, 1), jnp.float32)
    return pl.pallas_call(
        functools.partial(first_kernel, count),
        out_shape=(narrow, narrow, jax.ShapeDtypeStruct((rows, width), jnp.float32)),
        in_specs=[SMEM] + [VMEM] * (3 + count),
        out_specs=(VMEM, VMEM, VMEM),
        cost_estimate=attention_cost(rows, width, rows * (count + 1)),
        compiler_params=PARAMS,
        name="attend_first",
    )(bias, queries, keys, values, *blocks)


def attend_last(queries, state, blocks, bias):
    rows, width = queries.shape
    count = len(blocks)
    return pl.pallas_call(
        functools.partial(last_kernel, count),
        out_shape=jax.ShapeDtypeStruct((rows, width), jnp.bfloat16),
        in_specs=[SMEM] + [VMEM] * (4 + count),
        out_specs=VMEM,
        cost_estimate=attention_cost(rows, width, rows * count),
        compiler_params=PARAMS,
        name="attend_last",
    )(bias, queries, *state, *blocks)


def project_kernel(count, *refs):
    left, right, out_ref = refs[:count], refs[count : 2 * count], refs[2 * count]
    total = jnp.dot(left[0][...], right[0][...], preferred_element_type=jnp.float32)
    for a_ref, w_ref in zip(left[1:], right[1:]):
        total = total + jnp.dot(a_ref[...], w_ref[...], preferred_element_type=jnp.float32)
    out_ref[...] = total.astype(out_ref.dtype)


def project(pieces, weights):
    rows, depth = pieces[0].shape
    columns = weights[0].shape[1]
    tile = 256 if columns % 256 == 0 else columns
    count = len(pieces)
    return pl.pallas_call(
        functools.partial(project_kernel, count),
        grid=(columns // tile,),
        out_shape=jax.ShapeDtypeStruct((rows, columns), jnp.bfloat16),
        in_specs=[pl.BlockSpec((rows, depth), lambda c: (0, 0))] * count
        + [pl.BlockSpec((depth, tile), lambda c: (0, c))] * count,
        out_specs=pl.BlockSpec((rows, tile), lambda c: (0, c)),
        cost_estimate=pl.CostEstimate(
            flops=2 * count * rows * depth * columns,
            transcendentals=0,
            bytes_accessed=2 * count * depth * columns,
        ),
        compiler_params=PARAMS,
        name="project",
    )(*pieces, *weights)


def gather_blocks(block, count):
    half = count // 2
    direct, passed = [], []
    middle = None
    if half:
        right = [(i, i + half) for i in range(count - half)]
        left = [(i, i - half) for i in range(half, count)]
        if 2 * half == count:
            middle = lax.ppermute(block, "patch", right + left)
            direct.append((middle, 0, count))
            held_right = held_left = middle
        else:
            held_right = lax.ppermute(block, "patch", right)
            held_left = lax.ppermute(block, "patch", left)
            direct += [(held_right, half, count), (held_left, 0, count - half)]
    for step in range(1, half):
        right = [(i, i + step) for i in range(count - step)]
        left = [(i, i - step) for i in range(step, count)]
        direct.append((lax.ppermute(block, "patch", right), step, count))
        direct.append((lax.ppermute(block, "patch", left), 0, count - step))
    for distance in range(half + 1, count):
        step = distance - half
        right = [(i, i + step) for i in range(half, count - step)]
        left = [(i, i - step) for i in range(step, count - half)]
        if 2 * half == count:
            block_far = lax.ppermute(middle, "patch", right + left)
            passed.append((block_far, distance, count - distance))
        else:
            passed.append((lax.ppermute(held_right, "patch", right), distance, count))
            passed.append((lax.ppermute(held_left, "patch", left), 0, count - distance))
    return direct, passed


def bias_of(ranges):
    index = lax.axis_index("patch")
    rows = []
    for _, first, last in ranges:
        if first < last:
            valid = (index >= first) & (index < last)
        else:
            valid = (index >= first) | (index < last)
        rows.append(jnp.where(valid, 0.0, MASKED).astype(jnp.float32))
    return jnp.stack(rows)


def on_device(n_patch, n_head, queries, fresh_keys, fresh_values, stale_keys, stale_values, out_weight, gate_scale):
    ratio = n_patch // n_head
    assert n_patch == ratio * n_head and n_head & (n_head - 1) == 0

    both = jnp.concatenate([stale_keys, stale_values], axis=1)
    direct, passed = gather_blocks(both, n_patch)

    weights = [out_weight]
    far = []
    bit = n_head // 2
    while bit > 1:
        pairs = [(i, i ^ bit) for i in range(n_head)]
        far.append((bit, pairs))
        bit //= 2
    held = {0: out_weight}
    for bit, pairs in far:
        held.update({k ^ bit: lax.ppermute(w, "head", pairs) for k, w in list(held.items())})

    state = attend_first(
        queries, fresh_keys, fresh_values, [b for b, _, _ in direct], bias_of(direct)
    )
    attended = attend_last(queries, state, [b for b, _, _ in passed], bias_of(passed))

    def spread(i):
        return (i % 2) * (n_head // 2) + i // 2

    def slab_of(p, i, s):
        b, q = divmod(p, ratio)
        return ((q + s) % ratio) * n_head + (b + spread(i)) % n_head

    places = [(p, i) for p in range(n_patch) for i in range(n_head)]

    pieces = [
        [
            lax.ppermute(
                attended,
                ("patch", "head"),
                [(slab_of(p, i, s) * n_head + (i ^ t), p * n_head + i) for p, i in places],
            )
            for t in range(n_head)
        ]
        for s in range(ratio)
    ]

    if n_head > 1:
        pairs = [(i, i ^ 1) for i in range(n_head)]
        late, attended = lax.optimization_barrier((held, attended))
        held = dict(late)
        held.update({k ^ 1: lax.ppermute(w, "head", pairs) for k, w in list(held.items())})
    weights = [held[t] for t in range(n_head)]

    results = []
    for s in range(ratio):
        block = project(pieces[s], weights)
        results.append(
            lax.ppermute(
                block,
                ("patch", "head"),
                [(p * n_head + i, slab_of(p, i, s) * n_head + p // ratio) for p, i in places],
            )
        )
    if ratio == 1:
        rows = results[0]
    else:
        own = lax.axis_index("patch") // n_head
        stacked = jnp.stack(results)
        order = (own - jnp.arange(ratio)) % ratio
        rows = jnp.concatenate([stacked[order[k]] for k in range(ratio)], axis=1)
    return gate_scale[None, :] * rows.astype(jnp.float32)


def solution(mesh):
    return jax.shard_map(
        functools.partial(on_device, mesh.shape["patch"], mesh.shape["head"]),
        mesh=mesh,
        in_specs=(
            P(("groups", "patch"), "head"),
            P(("groups", "patch"), "head"),
            P(("groups", "patch"), "head"),
            P(("groups", "patch"), "head"),
            P(("groups", "patch"), "head"),
            P("head", "patch"),
            P(("groups", "head")),
        ),
        out_specs=P(("groups", "patch"), "head"),
        check_vma=False,
    )
```
